32 devices in a mesh: groups: 2 (over x), ctx: 4 (over y, core), head: 4 (over z).
Axes of the slice: x: 2, y: 2, z: 4, core: 2. Of those that a mesh axis runs over, the one named last changes fastest.
Arguments:
- queries: bfloat16 [256, 16384], P(('groups', 'ctx'), 'head'), parts along dimension 0, may hold values from -8 to 8
- cache_keys: bfloat16 [16384, 1024], P(('groups', 'ctx'), 'head'), parts along dimension 0, may hold values from -6 to 6
- cache_values: bfloat16 [16384, 1024], P(('groups', 'ctx'), 'head'), parts along dimension 0, may hold values from -6 to 6
- new_keys: bfloat16 [256, 1024], P(('groups', 'ctx'), 'head'), parts along dimension 0, may hold values from -8 to 8
- new_values: bfloat16 [256, 1024], P(('groups', 'ctx'), 'head'), parts along dimension 0, may hold values from -6 to 6
- out_weight: bfloat16 [16384, 16384], P('head', 'ctx'), may hold values from -0.1796875 to 0.1796875
- new_counts: int32 [8, 4], P('groups'), parts along dimension 0, may hold values from 1 to 16, 32 in all within a row
- cache_counts: int32 [8, 4], P('groups'), parts along dimension 0, may hold values from 1 to 512, 1536 in all within a row
- row_dest: int32 [256], P('groups'), parts along dimension 0, may hold values from 0 to 127, each once
Outputs:
- projected: bfloat16 [256, 16384], P(('groups', 'head'), 'ctx'), parts along dimension 0
The draws below stay inside these ranges and needn't reach their ends.
There are 2 independent parts, one for each index of `groups`. The reference program is written for one: setup_inputs(seed, part) draws one part's arguments, and reference() takes and returns one part's arrays. A program takes and returns all parts, laid end to end along the dimension named above; an argument that names none is the same for every part. Nothing has to cross between parts.
Inputs may be any that keep to these rules, and one draw needn't show every extreme that they name: Each row of new_counts sums to 32. `cache_counts`: each shard's counts sum to 1536. `row_dest`: each output row is named once.
All inputs are finite; a program needn't handle non-finite values.
Results may differ from the reference program's by a relative error of at most 0.017.
Values may be sent and summed in bfloat16 or wider, within the bound.
A program may use at most 128 MiB of HBM per device.

```python
import math
import jax
import jax.numpy as jnp
import numpy as np
from jax import lax

D = 16384
HEADS = 128
KV_HEADS = 8
HEAD_DIM = 128
Q_DEV = 32
CACHE_DEV = 2048
RPD = 4
GROUP = 16
TOKENS = 128
REQS = 4
CAPR = 512
N_CTX = 4


def draw_queries(key, part):
    shape = (TOKENS, HEADS * HEAD_DIM)
    base = jnp.clip(jax.random.normal(jax.random.fold_in(key, 21), shape, jnp.float32), -8.0, 8.0)
    return base.astype(jnp.bfloat16)


def draw_new_keys(key, part):
    shape = (TOKENS, KV_HEADS * HEAD_DIM)
    base = jnp.clip(jax.random.normal(jax.random.fold_in(key, 31), shape, jnp.float32), -8.0, 8.0)
    return base.astype(jnp.bfloat16)


def steps_of(rng, dims, pieces, low, high):
    loudness = 1.0
    for dim, blocks in pieces:
        heights = jax.random.uniform(jax.random.fold_in(jax.random.fold_in(rng, 6), dim), (blocks,), jnp.float32, low / len(pieces), high / len(pieces))
        loudness = loudness * jnp.repeat(jnp.exp(heights), dims[dim] // blocks).reshape((-1,) + (1,) * (len(dims) - 1 - dim))
    return loudness


def length_profile(amount, total, reach, lean):
    loads = [(1 << 20) // math.isqrt(rank ** lean) + 1 for rank in range(2, amount + 1)]
    rest, given = total - reach - (amount - 1), [1] * (amount - 1)
    while rest > 0:
        free = [i for i in range(amount - 1) if given[i] < reach]
        pool, budget = sum([loads[i] for i in free]), rest
        for i in free:
            more = min(reach - given[i], max(1, budget * loads[i] // pool), rest)
            given[i] = given[i] + more
            rest = rest - more
    return np.array([reach] + given)


def ragged(stream_key, number_of, total, limit, lean):
    if number_of == 2:
        one = jax.random.randint(stream_key, (), max(1, total - limit), min(limit, total - 1) + 1)
        return jnp.stack([one, total - one])
    tallies = jnp.asarray(length_profile(number_of, total, limit, lean), jnp.int32)
    pairs = (number_of - 1) // 2
    giver, receiver = tallies[1:1 + 2 * pairs:2], tallies[2:2 + 2 * pairs:2]
    margin = jnp.minimum(giver - 1, limit - receiver)
    moved = jax.random.randint(jax.random.fold_in(stream_key, 1), (pairs,), 0, 1 << 20) % (margin + 1)
    tallies = tallies.at[1:1 + 2 * pairs:2].set(giver - moved).at[2:2 + 2 * pairs:2].set(receiver + moved)
    return tallies[jax.random.permutation(jax.random.fold_in(stream_key, 2), number_of)]


def noise(key, dims, scale, limit, pieces=(), held_as=jnp.bfloat16):
    gain = steps_of(key, dims, pieces, -0.22, 0.18) if pieces else 1.0
    array = jax.random.normal(key, dims, jnp.float32) * scale * gain
    return jnp.minimum(jnp.maximum(array, -limit), limit).astype(held_as)


def setup_inputs(seed: int = 0, part: int = 0) -> dict:
    seeds = jax.random.split(jax.random.key(seed), 10)
    own_keys = jax.random.split(jax.random.fold_in(seeds[9], part), 10)
    return {
        "queries": draw_queries(jax.random.fold_in(jax.random.fold_in(seeds[9], part), 71), part),
        "cache_keys": noise(own_keys[1], (N_CTX * CACHE_DEV, KV_HEADS * HEAD_DIM), 1.0, 6.0, ((0, 4), (1, 4))),
        "cache_values": noise(own_keys[2], (N_CTX * CACHE_DEV, KV_HEADS * HEAD_DIM), 1.0, 6.0, ((0, 4), (1, 4))),
        "new_keys": draw_new_keys(jax.random.fold_in(jax.random.fold_in(seeds[9], part), 71), part),
        "new_values": noise(own_keys[4], (TOKENS, KV_HEADS * HEAD_DIM), 1.0, 6.0, ((0, 4), (1, 4))),
        "out_weight": noise(seeds[5], (HEADS * HEAD_DIM, D), 0.03, 0.1796875, ((0, 4), (1, 4))),
        "new_counts": jax.vmap(lambda own: ragged(own, RPD, Q_DEV, Q_DEV // 2, 2))(jax.random.split(own_keys[6], N_CTX)).reshape((N_CTX, RPD)).astype(jnp.int32),
        "cache_counts": jax.vmap(lambda own: ragged(own, REQS, CACHE_DEV * 3 // 4, CAPR, 2))(jax.random.split(own_keys[7], N_CTX)).reshape((N_CTX, REQS)).astype(jnp.int32),
        "row_dest": jax.random.permutation(own_keys[8], TOKENS).astype(jnp.int32),
    }


NEG = -1e+30

def row_requests(new_counts):
    ends = jnp.cumsum(new_counts, axis=1).astype(jnp.int32)
    offsets = jnp.arange(Q_DEV, dtype=jnp.int32)
    inside = lax.optimization_barrier(jnp.sum((offsets[None, :, None] >= ends[:, None, :]).astype(jnp.int32), axis=2))
    return inside.reshape(-1).astype(jnp.int32)

def cache_requests(cache_counts):
    ends = jnp.cumsum(cache_counts, axis=1).astype(jnp.int32)
    offsets = jnp.arange(CACHE_DEV, dtype=jnp.int32)
    return lax.optimization_barrier(jnp.sum((offsets[None, :, None] >= ends[:, None, :]).astype(jnp.int32), axis=2)).astype(jnp.int32)

def shard_partial(queries, query_req, query_pos, keys, values, key_req, key_pos):
    count = queries.shape[0]
    width = keys.shape[0]
    q_heads = queries.astype(jnp.float32).reshape(count, KV_HEADS, GROUP, HEAD_DIM)
    k_heads = keys.astype(jnp.float32).reshape(width, KV_HEADS, HEAD_DIM)
    v_heads = values.astype(jnp.float32).reshape(width, KV_HEADS, HEAD_DIM)
    scores = jnp.einsum('nhgd,khd->hngk', q_heads, k_heads) * (1.0 / math.sqrt(HEAD_DIM))
    visible = (key_req[None, :] == query_req[:, None]) & (key_pos[None, :] <= query_pos[:, None])
    visible = visible[None, :, None, :]
    top = lax.optimization_barrier(jnp.max(jnp.where(visible, scores, NEG), axis=3))
    probs = jnp.where(visible, jnp.exp(scores - top[..., None]), 0.0).astype(jnp.bfloat16)
    total = lax.optimization_barrier(jnp.sum(probs.astype(jnp.float32), axis=3))
    mixed = jnp.einsum('hngk,khd->nhgd', probs.astype(jnp.float32), v_heads)
    scale = jnp.maximum(total, 1.0).transpose(1, 0, 2)
    partial_value = (mixed / scale[..., None]).astype(jnp.bfloat16).reshape(count, -1)
    return (partial_value, top.transpose(1, 0, 2).reshape(count, -1), total.transpose(1, 0, 2).reshape(count, -1))

def reference(queries, cache_keys, cache_values, new_keys, new_values, out_weight, new_counts, cache_counts, row_dest):
    row_req = row_requests(new_counts)
    cache_req = cache_requests(cache_counts)
    positions = jnp.arange(TOKENS, dtype=jnp.int32)
    marks = jnp.full((CACHE_DEV,), -1, dtype=jnp.int32)

    def one_shard(items):
        shard_keys, shard_values, shard_req, fresh_keys, fresh_values, fresh_req, fresh_pos = items
        keys = jnp.concatenate([shard_keys, fresh_keys], axis=0)
        values = jnp.concatenate([shard_values, fresh_values], axis=0)
        key_req = jnp.concatenate([shard_req, fresh_req], axis=0).astype(jnp.int32)
        key_pos = jnp.concatenate([marks, fresh_pos], axis=0).astype(jnp.int32)
        return shard_partial(queries, row_req, positions, keys, values, key_req, key_pos)
    items = (cache_keys.reshape(N_CTX, CACHE_DEV, -1), cache_values.reshape(N_CTX, CACHE_DEV, -1), cache_req, new_keys.reshape(N_CTX, Q_DEV, -1), new_values.reshape(N_CTX, Q_DEV, -1), row_req.reshape(N_CTX, Q_DEV), positions.reshape(N_CTX, Q_DEV))
    partials, tops, totals = lax.map(one_shard, items)
    best = lax.optimization_barrier(jnp.max(tops, axis=0))
    weights = jnp.exp(tops - best[None]) * totals
    numer = lax.optimization_barrier(jnp.sum(weights[..., None] * partials.reshape(N_CTX, TOKENS, HEADS, HEAD_DIM).astype(jnp.float32), axis=0))
    attention = (numer / lax.optimization_barrier(jnp.sum(weights, axis=0))[..., None]).astype(jnp.bfloat16).reshape(TOKENS, -1)
    ordered = jnp.zeros_like(attention).at[row_dest].set(attention)
    return jnp.dot(ordered, out_weight, preferred_element_type=jnp.float32).astype(jnp.bfloat16)
```

```python
import functools
import math

import jax
import jax.numpy as jnp
from jax import lax
from jax.experimental import pallas as pl
from jax.experimental.pallas import tpu as pltpu
from jax.sharding import PartitionSpec as P

HEAD_DIM = 128
NEG = -1e30
MESH = pl.DeviceIdType.MESH
F32 = jnp.float32
BF16 = jnp.bfloat16


def tiles_of(total, width):
    return [(at, min(width, total - at)) for at in range(0, total, width)]


def parts_of(kv, grp):
    if kv % 2 == 0:
        return [[(h, 0, grp) for h in range(s * kv // 2, (s + 1) * kv // 2)] for s in range(2)]
    return [[(0, s * grp // 2, (s + 1) * grp // 2)] for s in range(2)]


def fused(
    n, nh, q_ref, ck_ref, cv_ref, nk_ref, nv_ref, w_ref, ncnt, ccnt, rd_ref, out_ref,
    q_all, kbuf, vbuf, bias, s_scr, part, stat, mpart, mstat, comb, cstat, xpart, xstat,
    att, order, wbuf, ybuf, rbuf, obuf,
    k_sem, v_sem, w_sem, own_sem, q_send, q_recv, m_send, m_recv, ms_send, ms_recv,
    x_send, x_recv, xs_send, xs_recv, a_send, a_recv, y_send, y_recv, o_sem,
):
    me = lax.axis_index("ctx")
    hz = lax.axis_index("head")
    core = lax.rem(me, 2)
    chip = lax.div(me, 2)
    chips = n // 2
    mate = chip * 2 + 1 - core
    rows = q_ref.shape[0]
    cached = ck_ref.shape[0] * 3 // 4
    keys = kbuf.shape[0]
    kv = ck_ref.shape[1] // HEAD_DIM
    grp = q_ref.shape[1] // HEAD_DIM // kv
    half = part.shape[3]
    heads = half // HEAD_DIM
    bands = rows // 8
    reqs = ncnt.shape[1]
    chunks, depth, cw = wbuf.shape
    orows = out_ref.shape[0]
    scale = 1.0 / math.sqrt(HEAD_DIM)
    scale2 = scale * math.log2(math.e)
    above = jnp.minimum(hz + 1, nh - 1)
    below = jnp.maximum(hz - 1, 0)

    barrier = pltpu.get_barrier_semaphore()
    pl.semaphore_signal(barrier, inc=1, device_id={"ctx": mate}, device_id_type=MESH)
    for d in range(1, chips):
        pl.semaphore_signal(
            barrier, inc=1, device_id={"ctx": lax.rem(me + 2 * d, n)}, device_id_type=MESH)

    @pl.when(hz < nh - 1)
    def _():
        pl.semaphore_signal(barrier, inc=1, device_id={"head": above}, device_id_type=MESH)

    @pl.when(hz > 0)
    def _():
        pl.semaphore_signal(barrier, inc=1, device_id={"head": below}, device_id_type=MESH)

    own = pltpu.make_async_copy(q_ref, q_all.at[me], own_sem)
    own.start()
    kcopies = [
        pltpu.make_async_copy(ck_ref.at[pl.ds(0, cached)], kbuf.at[pl.ds(0, cached)], k_sem.at[0]),
        pltpu.make_async_copy(nk_ref, kbuf.at[pl.ds(cached, rows)], k_sem.at[1]),
    ]
    for h in range(kv):
        cols = pl.ds(h * HEAD_DIM, HEAD_DIM)
        kcopies.append(pltpu.make_async_copy(
            cv_ref.at[pl.ds(0, cached), cols], vbuf.at[h, pl.ds(0, cached), pl.ds(0, HEAD_DIM)],
            v_sem.at[h, 0]))
        kcopies.append(pltpu.make_async_copy(
            nv_ref.at[:, cols], vbuf.at[h, pl.ds(cached, rows), pl.ds(0, HEAD_DIM)], v_sem.at[h, 1]))
    for copy in kcopies:
        copy.start()

    def wcopy(c):
        return pltpu.make_async_copy(
            w_ref.at[:, pl.ds(pl.multiple_of(c * cw, cw), cw)], wbuf.at[c], w_sem.at[c])

    pad = keys - cached - rows
    kbuf[pl.ds(cached + rows, pad), :] = jnp.zeros((pad, kbuf.shape[1]), BF16)
    for h in range(kv):
        vbuf[h, pl.ds(cached + rows, pad), pl.ds(0, HEAD_DIM)] = jnp.zeros((pad, HEAD_DIM), BF16)
        vbuf[h, :, pl.ds(HEAD_DIM, HEAD_DIM)] = jnp.ones((keys, HEAD_DIM), BF16)

    pl.semaphore_wait(
        barrier, chips + (hz < nh - 1).astype(jnp.int32) + (hz > 0).astype(jnp.int32))

    def to_ctx(src, dst, send, recv, to):
        return pltpu.make_async_remote_copy(
            src_ref=src, dst_ref=dst, send_sem=send, recv_sem=recv,
            device_id={"ctx": to}, device_id_type=MESH)

    def twin(d):
        return lax.rem(chip + d, chips) * 2 + core

    def q_out(k):
        return to_ctx(q_ref, q_all.at[me], q_send.at[2 * k], q_recv.at[2 * k], twin(chips - k))

    q_mate = to_ctx(q_ref, q_all.at[me], q_send.at[1], q_recv.at[1], mate)
    for k in range(1, chips):
        q_out(k).start()
    q_mate.start()

    def block_of(i):
        return lax.rem(chip + lax.div(i, 2), chips) * 2 + lax.rem(core + i, 2)

    def q_in(i):
        b = block_of(i)
        return to_ctx(q_all.at[b], q_all.at[b], q_send.at[i], q_recv.at[i], mate)

    def q_pass(i):
        b = block_of(i)
        return to_ctx(q_all.at[b], q_all.at[b], q_send.at[i + 1], q_recv.at[i + 1], mate)

    def start_w(c, _):
        wcopy(c).start()
        return 0

    lax.fori_loop(0, chunks, start_w, 0)

    lane = lax.broadcasted_iota(jnp.int32, (1, keys), 1)
    key_req = jnp.zeros((1, keys), jnp.int32)
    edge = jnp.int32(0)
    for r in range(reqs):
        edge = edge + ccnt[me, r]
        key_req = key_req + (lane >= edge).astype(jnp.int32)
    fresh = lane - cached
    fresh_req = jnp.zeros((1, keys), jnp.int32)
    edge = jnp.int32(0)
    for r in range(reqs):
        edge = edge + ncnt[me, r]
        fresh_req = fresh_req + (fresh >= edge).astype(jnp.int32)
    key_req = jnp.where(lane >= cached, jnp.where(fresh < rows, fresh_req, -1), key_req)
    key_pos = jnp.where(lane >= cached, me * rows + fresh, -1)

    for copy in kcopies:
        copy.wait()
    own.wait()

    def mate_part(b):
        return to_ctx(part.at[b, 1 - core], mpart.at[b], m_send.at[b], m_recv.at[b], mate)

    def mate_stat(b):
        return to_ctx(stat.at[b, 1 - core], mstat.at[b], ms_send.at[b], ms_recv.at[b], mate)

    def chip_part(b, d):
        return to_ctx(comb.at[b], xpart.at[d - 1, b], x_send.at[d - 1, b], x_recv.at[d - 1, b], twin(d))

    def chip_stat(b, d):
        return to_ctx(cstat.at[b], xstat.at[d - 1, b], xs_send.at[d - 1, b], xs_recv.at[d - 1, b], twin(d))

    def att_part(b, side):
        return to_ctx(att.at[b, side], att.at[b, side], a_send.at[b], a_recv.at[b], mate)

    def spread(weight, e):
        return jnp.concatenate(
            [jnp.broadcast_to(weight[:, r * heads + e:r * heads + e + 1], (8, HEAD_DIM))
             for r in range(bands)], axis=0)

    def blend(pieces, stats, store):
        best = functools.reduce(jnp.maximum, stats)
        weights = [jnp.exp(item - best) for item in stats]
        whole = functools.reduce(jnp.add, weights)
        weights = [item / whole for item in weights]
        for e in range(heads):
            cols = slice(e * HEAD_DIM, (e + 1) * HEAD_DIM)
            terms = [spread(w, e) * piece[:, cols].astype(F32) for w, piece in zip(weights, pieces)]
            store(cols, functools.reduce(jnp.add, terms).astype(BF16))
        return best + jnp.log(whole)

    def combine(b):
        mate_stat(b).wait_recv()
        mate_part(b).wait_recv()

        def store(cols, value):
            comb[b, :, cols] = value

        cstat[b] = blend([part.at[b, core], mpart.at[b]], [stat[b, core], mstat[b]], store)
        for d in range(1, chips):
            chip_stat(b, d).start()
            chip_part(b, d).start()

    def conclude(b):
        for d in range(1, chips):
            chip_stat(b, d).wait_recv()
            chip_part(b, d).wait_recv()

        def store(cols, value):
            att[b, core, :, cols] = value

        blend([comb.at[b]] + [xpart.at[d - 1, b] for d in range(1, chips)],
              [cstat[b]] + [xstat[d - 1, b] for d in range(1, chips)], store)
        att_part(b, core).start()

    spans = tiles_of(keys, 512)
    band_lane = lax.broadcasted_iota(jnp.int32, (8, HEAD_DIM), 1)

    def step(i, _):
        b = block_of(i)

        @pl.when(i > 0)
        def _():
            q_in(i).wait_recv()

        @pl.when((i > 0) & (lax.rem(i, 2) == 0))
        def _():
            q_pass(i).start()

        row = lax.broadcasted_iota(jnp.int32, (rows, 1), 0)
        row_req = jnp.zeros((rows, 1), jnp.int32)
        edge = jnp.int32(0)
        for r in range(reqs):
            edge = edge + ncnt[b, r]
            row_req = row_req + (row >= edge).astype(jnp.int32)
        seen = (key_req == row_req) & (key_pos <= b * rows + row)
        bias[...] = jnp.where(seen, 0.0, NEG)

        slot = 0
        for side, items in enumerate(parts_of(kv, grp)):
            packed = jnp.zeros((8, HEAD_DIM), F32)
            e = 0
            for h, first, last in items:
                count = last - first
                q = jnp.concatenate(
                    [q_all[b, :, (h * grp + g) * HEAD_DIM:(h * grp + g + 1) * HEAD_DIM]
                     for g in range(first, last)], axis=0)
                most = None
                for at, size in spans:
                    s = lax.dot_general(
                        q, kbuf[at:at + size, h * HEAD_DIM:(h + 1) * HEAD_DIM],
                        (((1,), (1,)), ((), ())), preferred_element_type=F32)
                    s = (s.reshape(count, rows, size) + bias[:, at:at + size][None]).reshape(count * rows, size)
                    s_scr[slot, :, at:at + size] = s
                    for j in range(0, size, HEAD_DIM):
                        piece = s[:, j:j + HEAD_DIM]
                        most = piece if most is None else jnp.maximum(most, piece)
                top = jnp.max(most, axis=1, keepdims=True)
                shift = top * scale2
                acc = None
                for at, size in spans:
                    p = jnp.exp2(s_scr[slot, :, at:at + size] * scale2 - shift).astype(BF16)
                    term = jnp.dot(p, vbuf[h, at:at + size, :], preferred_element_type=F32)
                    acc = term if acc is None else acc + term
                total = acc[:, HEAD_DIM:]
                value = (acc[:, :HEAD_DIM] / jnp.maximum(total, 1.0)).astype(BF16)
                lse = jnp.where(top > 0.5 * NEG, top * scale + jnp.log(jnp.maximum(total, 1.0)), NEG)
                for g in range(count):
                    part[b, side, :, e * HEAD_DIM:(e + 1) * HEAD_DIM] = value[g * rows:(g + 1) * rows]
                    for r in range(bands):
                        packed = jnp.where(
                            band_lane == r * heads + e, lse[g * rows + r * 8:g * rows + r * 8 + 8], packed)
                    e += 1
                slot += 1
            stat[b, side] = packed

        mate_stat(b).start()
        mate_part(b).start()

        @pl.when(lax.rem(i, 2) == 1)
        def _():
            combine(b)
            combine(block_of(i - 1))
        return 0

    lax.fori_loop(0, n, step, 0)

    def close(j, _):
        conclude(block_of(n - 1 - j))
        return 0

    lax.fori_loop(0, n, close, 0)

    everyone = n * rows
    pick = (lax.broadcasted_iota(jnp.int32, (everyone, everyone), 0) == rd_ref[...]).astype(F32).astype(BF16)

    def arrange(side):
        for at, size in tiles_of(half, 1024):
            order[:, pl.ds(pl.multiple_of(side * half + at, HEAD_DIM), size)] = jnp.dot(
                pick, att[:, side, :, at:at + size].reshape(everyone, size),
                preferred_element_type=F32).astype(BF16)

    arrange(core)
    for b in range(n):
        att_part(b, 1 - core).wait_recv()
    arrange(1 - core)

    def columns(c):
        return pl.ds(pl.multiple_of(c * cw, cw), cw)

    def share(t):
        return pl.ds(t * orows, orows)

    def up(c, t):
        return pltpu.make_async_remote_copy(
            src_ref=ybuf.at[share(t), columns(c)], dst_ref=rbuf.at[t, :, columns(c)],
            send_sem=y_send.at[t, c], recv_sem=y_recv.at[t, c],
            device_id={"head": above}, device_id_type=MESH)

    def down(c, t):
        slot = jnp.where(hz - 1 == t, nh, t)
        return pltpu.make_async_remote_copy(
            src_ref=ybuf.at[share(t), columns(c)], dst_ref=rbuf.at[slot, :, columns(c)],
            send_sem=y_send.at[t, c], recv_sem=y_recv.at[slot, c],
            device_id={"head": below}, device_id_type=MESH)

    def arrived(c, slot):
        return pltpu.make_async_remote_copy(
            src_ref=rbuf.at[slot, :, columns(c)], dst_ref=rbuf.at[slot, :, columns(c)],
            send_sem=y_send.at[slot, c], recv_sem=y_recv.at[slot, c],
            device_id={"head": above}, device_id_type=MESH)

    def add_arrived(c, t):
        arrived(c, t).wait_recv()
        cols = columns(c)
        ybuf[share(t), cols] = (ybuf[share(t), cols].astype(F32) + rbuf[t, :, cols].astype(F32)).astype(BF16)

    def project(k, _):
        @pl.when(k < chunks)
        def _():
            wcopy(k).wait()
            ybuf[:, columns(k)] = jnp.dot(
                order[...], wbuf[k], preferred_element_type=F32).astype(BF16)

        rise = k - hz
        fall = k - (nh - 1 - hz)
        for t in reversed(range(1, nh)):
            @pl.when((rise >= 0) & (rise < chunks) & (hz == 0) & (t > 1))
            def _():
                up(rise, t).start()

            @pl.when((rise >= 0) & (rise < chunks) & (hz > 0) & (t > hz))
            def _():
                add_arrived(rise, t)
                up(rise, t).start()

        for t in range(nh - 1):
            @pl.when((fall >= 0) & (fall < chunks) & (hz == nh - 1) & (t < nh - 2))
            def _():
                down(fall, t).start()

            @pl.when((fall >= 0) & (fall < chunks) & (hz < nh - 1) & (t < hz))
            def _():
                add_arrived(fall, t)
                down(fall, t).start()

        @pl.when(k == chunks - 1)
        def _():
            def near(c, _):
                @pl.when(hz == 0)
                def _():
                    up(c, 1).start()

                @pl.when(hz == nh - 1)
                def _():
                    down(c, nh - 2).start()
                return 0

            lax.fori_loop(0, chunks, near, 0)
        return 0

    lax.fori_loop(0, chunks + nh - 2, project, 0)

    def leave(c):
        return pltpu.make_async_copy(obuf.at[:, columns(c)], out_ref.at[:, columns(c)], o_sem.at[c])

    def finish(c, _):
        cols = columns(c)
        mine = pl.ds(pl.multiple_of(hz * orows, orows), orows)

        @pl.when(hz == 0)
        def _():
            arrived(c, nh).wait_recv()
            obuf[:, cols] = (ybuf[mine, cols].astype(F32) + rbuf[nh, :, cols].astype(F32)).astype(BF16)

        @pl.when(hz == nh - 1)
        def _():
            arrived(c, hz).wait_recv()
            obuf[:, cols] = (ybuf[mine, cols].astype(F32) + rbuf[hz, :, cols].astype(F32)).astype(BF16)

        @pl.when((hz > 0) & (hz < nh - 1))
        def _():
            arrived(c, hz).wait_recv()
            arrived(c, nh).wait_recv()
            obuf[:, cols] = (ybuf[mine, cols].astype(F32) + rbuf[hz, :, cols].astype(F32)
                             + rbuf[nh, :, cols].astype(F32)).astype(BF16)

        leave(c).start()
        return 0

    lax.fori_loop(0, chunks, finish, 0)

    for k in range(1, chips):
        q_out(k).wait_send()
        q_pass(jnp.int32(2 * k)).wait_send()
    q_mate.wait_send()

    def drain(b, _):
        mate_stat(b).wait_send()
        mate_part(b).wait_send()
        att_part(b, core).wait_send()
        for d in range(1, chips):
            chip_stat(b, d).wait_send()
            chip_part(b, d).wait_send()
        return 0

    lax.fori_loop(0, n, drain, 0)

    def drain_y(c, _):
        for t in range(nh):
            @pl.when(t != hz)
            def _():
                up(c, t).wait_send()
        leave(c).wait()
        return 0

    lax.fori_loop(0, chunks, drain_y, 0)


def per_device(
    n, nh, queries, cache_keys, cache_values, new_keys, new_values, out_weight,
    new_counts, cache_counts, row_dest,
):
    rows, width = queries.shape
    cached, kvw = cache_keys.shape
    kv = kvw // HEAD_DIM
    grp = width // kvw
    depth, cols = out_weight.shape
    keys = cached * 3 // 4 + -(-rows // HEAD_DIM) * HEAD_DIM
    everyone = n * rows
    orows = everyone // nh
    chips = n // 2
    half = width // 2
    plan = parts_of(kv, grp)
    slots = sum(len(items) for items in plan)
    tall = (plan[0][0][2] - plan[0][0][1]) * rows
    cw = 1024 if cols % 1024 == 0 else HEAD_DIM
    chunks = cols // cw
    dma = pltpu.SemaphoreType.DMA
    hbm = pl.BlockSpec(memory_space=pl.ANY)
    smem = pl.BlockSpec(memory_space=pltpu.SMEM)
    vmem = pl.BlockSpec(memory_space=pltpu.VMEM)
    return pl.pallas_call(
        functools.partial(fused, n, nh),
        out_shape=jax.ShapeDtypeStruct((orows, cols), BF16),
        in_specs=[hbm] * 6 + [smem] * 2 + [vmem],
        out_specs=hbm,
        scratch_shapes=[
            pltpu.VMEM((n, rows, width), BF16),
            pltpu.VMEM((keys, kvw), BF16),
            pltpu.VMEM((kv, keys, 2 * HEAD_DIM), BF16),
            pltpu.VMEM((rows, keys), F32),
            pltpu.VMEM((slots, tall, keys), F32),
            pltpu.VMEM((n, 2, rows, half), BF16),
            pltpu.VMEM((n, 2, 8, HEAD_DIM), F32),
            pltpu.VMEM((n, rows, half), BF16),
            pltpu.VMEM((n, 8, HEAD_DIM), F32),
            pltpu.VMEM((n, rows, half), BF16),
            pltpu.VMEM((n, 8, HEAD_DIM), F32),
            pltpu.VMEM((chips - 1, n, rows, half), BF16),
            pltpu.VMEM((chips - 1, n, 8, HEAD_DIM), F32),
            pltpu.VMEM((n, 2, rows, half), BF16),
            pltpu.VMEM((everyone, width), BF16),
            pltpu.VMEM((chunks, depth, cw), BF16),
            pltpu.VMEM((everyone, cols), BF16),
            pltpu.VMEM((nh + 1, orows, cols), BF16),
            pltpu.VMEM((orows, cols), BF16),
            dma((2,)), dma((kv, 2)), dma((chunks,)), dma,
            dma((n,)), dma((n,)),
            dma((n,)), dma((n,)), dma((n,)), dma((n,)),
            dma((chips - 1, n)), dma((chips - 1, n)), dma((chips - 1, n)), dma((chips - 1, n)),
            dma((n,)), dma((n,)),
            dma((nh + 1, chunks)), dma((nh + 1, chunks)), dma((chunks,)),
        ],
        compiler_params=pltpu.CompilerParams(
            collective_id=0, has_side_effects=True, vmem_limit_bytes=60 * 1024 * 1024),
    )(queries, cache_keys, cache_values, new_keys, new_values, out_weight,
      new_counts, cache_counts, row_dest.reshape(1, everyone))


def solution(mesh):
    n, nh = mesh.shape["ctx"], mesh.shape["head"]
    return jax.shard_map(
        functools.partial(per_device, n, nh),
        mesh=mesh,
        in_specs=(
            P(("groups", "ctx"), "head"),
            P(("groups", "ctx"), "head"),
            P(("groups", "ctx"), "head"),
            P(("groups", "ctx"), "head"),
            P(("groups", "ctx"), "head"),
            P("head", "ctx"),
            P("groups", None),
            P("groups", None),
            P("groups"),
        ),
        out_specs=P(("groups", "head"), "ctx"),
        check_vma=False,
    )
```

```python
import functools
import math

import jax
import jax.numpy as jnp
from jax import lax
from jax.experimental import pallas as pl
from jax.experimental.pallas import tpu as pltpu
from jax.sharding import PartitionSpec as P

HEAD_DIM = 128
NEG = -1e30
MESH = pl.DeviceIdType.MESH
F32 = jnp.float32
BF16 = jnp.bfloat16


def tiles_of(total, width):
    return [(at, min(width, total - at)) for at in range(0, total, width)]


def parts_of(kv, grp):
    if kv % 2 == 0:
        return [[(h, 0, grp) for h in range(s * kv // 2, (s + 1) * kv // 2)] for s in range(2)]
    return [[(0, s * grp // 2, (s + 1) * grp // 2)] for s in range(2)]


def fused(
    n, nh, q_ref, ck_ref, cv_ref, nk_ref, nv_ref, w_ref, ncnt, ccnt, rd_ref, out_ref,
    q_all, kbuf, vbuf, bias, s_scr, part, stat, mpart, mstat, comb, cstat, xpart, xstat,
    att, order, wbuf, start, ybuf, rbuf, obuf,
    k_sem, v_sem, w_sem, own_sem, q_send, q_recv, m_send, m_recv, ms_send, ms_recv,
    x_send, x_recv, xs_send, xs_recv, a_send, a_recv, y_send, y_recv, o_sem,
):
    me = lax.axis_index("ctx")
    hz = lax.axis_index("head")
    core = lax.rem(me, 2)
    chip = lax.div(me, 2)
    chips = n // 2
    mate = chip * 2 + 1 - core
    rows = q_ref.shape[0]
    cached = ck_ref.shape[0] * 3 // 4
    keys = kbuf.shape[0]
    kv = ck_ref.shape[1] // HEAD_DIM
    grp = q_ref.shape[1] // HEAD_DIM // kv
    half = part.shape[3]
    heads = half // HEAD_DIM
    bands = rows // 8
    reqs = ncnt.shape[1]
    chunks, depth, cw = wbuf.shape
    orows = out_ref.shape[0]
    scale = 1.0 / math.sqrt(HEAD_DIM)
    scale2 = scale * math.log2(math.e)
    above = jnp.minimum(hz + 1, nh - 1)
    below = jnp.maximum(hz - 1, 0)

    barrier = pltpu.get_barrier_semaphore()
    pl.semaphore_signal(barrier, inc=1, device_id={"ctx": mate}, device_id_type=MESH)
    for d in range(1, chips):
        pl.semaphore_signal(
            barrier, inc=1, device_id={"ctx": lax.rem(me + 2 * d, n)}, device_id_type=MESH)

    @pl.when(hz < nh - 1)
    def _():
        pl.semaphore_signal(barrier, inc=1, device_id={"head": above}, device_id_type=MESH)

    @pl.when(hz > 0)
    def _():
        pl.semaphore_signal(barrier, inc=1, device_id={"head": below}, device_id_type=MESH)

    own = pltpu.make_async_copy(q_ref, q_all.at[me], own_sem)
    own.start()
    kcopies = [
        pltpu.make_async_copy(ck_ref.at[pl.ds(0, cached)], kbuf.at[pl.ds(0, cached)], k_sem.at[0]),
        pltpu.make_async_copy(nk_ref, kbuf.at[pl.ds(cached, rows)], k_sem.at[1]),
    ]
    for h in range(kv):
        cols = pl.ds(h * HEAD_DIM, HEAD_DIM)
        kcopies.append(pltpu.make_async_copy(
            cv_ref.at[pl.ds(0, cached), cols], vbuf.at[h, pl.ds(0, cached), pl.ds(0, HEAD_DIM)],
            v_sem.at[h, 0]))
        kcopies.append(pltpu.make_async_copy(
            nv_ref.at[:, cols], vbuf.at[h, pl.ds(cached, rows), pl.ds(0, HEAD_DIM)], v_sem.at[h, 1]))
    for copy in kcopies:
        copy.start()

    def wcopy(c):
        return pltpu.make_async_copy(
            w_ref.at[:, pl.ds(pl.multiple_of(c * cw, cw), cw)], wbuf.at[c], w_sem.at[c])

    pad = keys - cached - rows
    kbuf[pl.ds(cached + rows, pad), :] = jnp.zeros((pad, kbuf.shape[1]), BF16)
    for h in range(kv):
        vbuf[h, pl.ds(cached + rows, pad), pl.ds(0, HEAD_DIM)] = jnp.zeros((pad, HEAD_DIM), BF16)
        vbuf[h, :, pl.ds(HEAD_DIM, HEAD_DIM)] = jnp.ones((keys, HEAD_DIM), BF16)

    pl.semaphore_wait(
        barrier, chips + (hz < nh - 1).astype(jnp.int32) + (hz > 0).astype(jnp.int32))

    def to_ctx(src, dst, send, recv, to):
        return pltpu.make_async_remote_copy(
            src_ref=src, dst_ref=dst, send_sem=send, recv_sem=recv,
            device_id={"ctx": to}, device_id_type=MESH)

    def twin(d):
        return lax.rem(chip + d, chips) * 2 + core

    def q_out(k):
        return to_ctx(q_ref, q_all.at[me], q_send.at[2 * k], q_recv.at[2 * k], twin(chips - k))

    q_mate = to_ctx(q_ref, q_all.at[me], q_send.at[1], q_recv.at[1], mate)
    for k in range(1, chips):
        q_out(k).start()
    q_mate.start()

    def block_of(i):
        return lax.rem(chip + lax.div(i, 2), chips) * 2 + lax.rem(core + i, 2)

    def q_in(i):
        b = block_of(i)
        return to_ctx(q_all.at[b], q_all.at[b], q_send.at[i], q_recv.at[i], mate)

    def q_pass(i):
        b = block_of(i)
        return to_ctx(q_all.at[b], q_all.at[b], q_send.at[i + 1], q_recv.at[i + 1], mate)

    def start_w(c, _):
        wcopy(c).start()
        return 0

    lax.fori_loop(0, chunks, start_w, 0)

    lane = lax.broadcasted_iota(jnp.int32, (1, keys), 1)
    key_req = jnp.zeros((1, keys), jnp.int32)
    edge = jnp.int32(0)
    for r in range(reqs):
        edge = edge + ccnt[me, r]
        key_req = key_req + (lane >= edge).astype(jnp.int32)
    fresh = lane - cached
    fresh_req = jnp.zeros((1, keys), jnp.int32)
    edge = jnp.int32(0)
    for r in range(reqs):
        edge = edge + ncnt[me, r]
        fresh_req = fresh_req + (fresh >= edge).astype(jnp.int32)
    key_req = jnp.where(lane >= cached, jnp.where(fresh < rows, fresh_req, -1), key_req)
    key_pos = jnp.where(lane >= cached, me * rows + fresh, -1)

    for copy in kcopies:
        copy.wait()
    own.wait()

    def mate_part(b):
        return to_ctx(part.at[b, 1 - core], mpart.at[b], m_send.at[b], m_recv.at[b], mate)

    def mate_stat(b):
        return to_ctx(stat.at[b, 1 - core], mstat.at[b], ms_send.at[b], ms_recv.at[b], mate)

    def chip_part(b, d):
        return to_ctx(comb.at[b], xpart.at[d - 1, b], x_send.at[d - 1, b], x_recv.at[d - 1, b], twin(d))

    def chip_stat(b, d):
        return to_ctx(cstat.at[b], xstat.at[d - 1, b], xs_send.at[d - 1, b], xs_recv.at[d - 1, b], twin(d))

    def att_part(b, side):
        return to_ctx(att.at[b, side], att.at[b, side], a_send.at[b], a_recv.at[b], mate)

    band_lane = lax.broadcasted_iota(jnp.int32, (8, HEAD_DIM), 1)

    def spread(weight, e):
        return jnp.concatenate(
            [jnp.broadcast_to(weight[:, r * heads + e:r * heads + e + 1], (8, HEAD_DIM))
             for r in range(bands)], axis=0)

    def blend(pieces, stats, store, last):
        best = functools.reduce(jnp.maximum, stats)
        weights = [jnp.exp(item - best) for item in stats]
        wide = [pltpu.roll(item, HEAD_DIM // 2, 1) for item in weights]
        whole = functools.reduce(jnp.add, [w * item for w, item in zip(wide, stats)])
        if last:
            share = 1.0 / pltpu.roll(whole, HEAD_DIM // 2, 1)
            weights = [item * share for item in weights]
        for e in range(heads):
            cols = slice(e * HEAD_DIM, (e + 1) * HEAD_DIM)
            terms = [spread(w, e) * piece[:, cols].astype(F32) for w, piece in zip(weights, pieces)]
            store(cols, functools.reduce(jnp.add, terms).astype(BF16))
        return jnp.where(band_lane < HEAD_DIM // 2, best, whole)

    def combine(b):
        mate_stat(b).wait_recv()
        mate_part(b).wait_recv()

        def store(cols, value):
            comb[b, :, cols] = value

        cstat[b] = blend([part.at[b, core], mpart.at[b]], [stat[b, core], mstat[b]], store, False)
        for d in range(1, chips):
            chip_stat(b, d).start()
            chip_part(b, d).start()

    def conclude(b):
        for d in range(1, chips):
            chip_stat(b, d).wait_recv()
            chip_part(b, d).wait_recv()

        def store(cols, value):
            att[b, core, :, cols] = value

        blend([comb.at[b]] + [xpart.at[d - 1, b] for d in range(1, chips)],
              [cstat[b]] + [xstat[d - 1, b] for d in range(1, chips)], store, True)
        att_part(b, core).start()

    spans = tiles_of(keys, 512)

    def step(i, _):
        b = block_of(i)

        @pl.when(i > 0)
        def _():
            q_in(i).wait_recv()

        @pl.when((i > 0) & (lax.rem(i, 2) == 0))
        def _():
            q_pass(i).start()

        row = lax.broadcasted_iota(jnp.int32, (rows, 1), 0)
        row_req = jnp.zeros((rows, 1), jnp.int32)
        edge = jnp.int32(0)
        for r in range(reqs):
            edge = edge + ncnt[b, r]
            row_req = row_req + (row >= edge).astype(jnp.int32)
        seen = (key_req == row_req) & (key_pos <= b * rows + row)
        bias[...] = jnp.where(seen, 0.0, NEG)

        slot = 0
        for side, items in enumerate(parts_of(kv, grp)):
            packed = jnp.zeros((8, HEAD_DIM), F32)
            e = 0
            for h, first, last in items:
                count = last - first
                q = jnp.concatenate(
                    [q_all[b, :, (h * grp + g) * HEAD_DIM:(h * grp + g + 1) * HEAD_DIM]
                     for g in range(first, last)], axis=0)
                most = None
                for at, size in spans:
                    s = lax.dot_general(
                        q, kbuf[at:at + size, h * HEAD_DIM:(h + 1) * HEAD_DIM],
                        (((1,), (1,)), ((), ())), preferred_element_type=F32)
                    s = (s.reshape(count, rows, size) + bias[:, at:at + size][None]).reshape(count * rows, size)
                    s_scr[slot, :, at:at + size] = s
                    for j in range(0, size, HEAD_DIM):
                        piece = s[:, j:j + HEAD_DIM]
                        most = piece if most is None else jnp.maximum(most, piece)
                top = jnp.max(most, axis=1, keepdims=True)
                shift = top * scale2
                acc = None
                for at, size in spans:
                    p = jnp.exp2(s_scr[slot, :, at:at + size] * scale2 - shift).astype(BF16)
                    term = jnp.dot(p, vbuf[h, at:at + size, :], preferred_element_type=F32)
                    acc = term if acc is None else acc + term
                total = acc[:, HEAD_DIM:]
                value = acc[:, :HEAD_DIM].astype(BF16)
                most = jnp.broadcast_to(top, (count * rows, HEAD_DIM))
                for g in range(count):
                    part[b, side, :, e * HEAD_DIM:(e + 1) * HEAD_DIM] = value[g * rows:(g + 1) * rows]
                    for r in range(bands):
                        band = slice(g * rows + r * 8, g * rows + r * 8 + 8)
                        packed = jnp.where(band_lane == r * heads + e, most[band], packed)
                        packed = jnp.where(band_lane == HEAD_DIM // 2 + r * heads + e, total[band], packed)
                    e += 1
                slot += 1
            stat[b, side] = jnp.where(band_lane < HEAD_DIM // 2, packed * scale, packed)

        mate_stat(b).start()
        mate_part(b).start()

        @pl.when(lax.rem(i, 2) == 1)
        def _():
            combine(b)
            combine(block_of(i - 1))
        return 0

    lax.fori_loop(0, n, step, 0)

    def close(j, _):
        conclude(block_of(n - 1 - j))
        return 0

    lax.fori_loop(0, n, close, 0)

    everyone = n * rows
    pick = (lax.broadcasted_iota(jnp.int32, (everyone, everyone), 0) == rd_ref[...]).astype(F32).astype(BF16)

    def arrange(side):
        for at, size in tiles_of(half, 1024):
            order[:, pl.ds(pl.multiple_of(side * half + at, HEAD_DIM), size)] = jnp.dot(
                pick, att[:, side, :, at:at + size].reshape(everyone, size),
                preferred_element_type=F32).astype(BF16)

    def first_chunk(side):
        at = pl.ds(pl.multiple_of(side * half, HEAD_DIM), half)
        return jnp.dot(order[:, at], wbuf[0, at, :], preferred_element_type=F32)

    arrange(core)
    wcopy(0).wait()
    start[...] = first_chunk(core)
    for b in range(n):
        att_part(b, 1 - core).wait_recv()
    arrange(1 - core)
    ybuf[:, pl.ds(0, cw)] = (start[...] + first_chunk(1 - core)).astype(BF16)

    def columns(c):
        return pl.ds(pl.multiple_of(c * cw, cw), cw)

    def share(t):
        return pl.ds(t * orows, orows)

    def up(c, t):
        return pltpu.make_async_remote_copy(
            src_ref=ybuf.at[share(t), columns(c)], dst_ref=rbuf.at[t, :, columns(c)],
            send_sem=y_send.at[t, c], recv_sem=y_recv.at[t, c],
            device_id={"head": above}, device_id_type=MESH)

    def down(c, t):
        slot = jnp.where(hz - 1 == t, nh, t)
        return pltpu.make_async_remote_copy(
            src_ref=ybuf.at[share(t), columns(c)], dst_ref=rbuf.at[slot, :, columns(c)],
            send_sem=y_send.at[t, c], recv_sem=y_recv.at[slot, c],
            device_id={"head": below}, device_id_type=MESH)

    def arrived(c, slot):
        return pltpu.make_async_remote_copy(
            src_ref=rbuf.at[slot, :, columns(c)], dst_ref=rbuf.at[slot, :, columns(c)],
            send_sem=y_send.at[slot, c], recv_sem=y_recv.at[slot, c],
            device_id={"head": above}, device_id_type=MESH)

    def add_arrived(c, t):
        arrived(c, t).wait_recv()
        cols = columns(c)
        ybuf[share(t), cols] = (ybuf[share(t), cols].astype(F32) + rbuf[t, :, cols].astype(F32)).astype(BF16)

    def project(k, _):
        @pl.when((k > 0) & (k < chunks))
        def _():
            wcopy(k).wait()
            ybuf[:, columns(k)] = jnp.dot(
                order[...], wbuf[k], preferred_element_type=F32).astype(BF16)

        rise = k - hz
        fall = k - (nh - 1 - hz)
        for t in reversed(range(1, nh)):
            @pl.when((rise >= 0) & (rise < chunks) & (hz == 0) & (t > 1))
            def _():
                up(rise, t).start()

            @pl.when((rise >= 0) & (rise < chunks) & (hz > 0) & (t > hz))
            def _():
                add_arrived(rise, t)
                up(rise, t).start()

        for t in range(nh - 1):
            @pl.when((fall >= 0) & (fall < chunks) & (hz == nh - 1) & (t < nh - 2))
            def _():
                down(fall, t).start()

            @pl.when((fall >= 0) & (fall < chunks) & (hz < nh - 1) & (t < hz))
            def _():
                add_arrived(fall, t)
                down(fall, t).start()

        @pl.when(k == chunks - 1)
        def _():
            def near(c, _):
                @pl.when(hz == 0)
                def _():
                    up(c, 1).start()

                @pl.when(hz == nh - 1)
                def _():
                    down(c, nh - 2).start()
                return 0

            lax.fori_loop(0, chunks, near, 0)
        return 0

    lax.fori_loop(0, chunks + nh - 2, project, 0)

    def leave(c):
        return pltpu.make_async_copy(obuf.at[:, columns(c)], out_ref.at[:, columns(c)], o_sem.at[c])

    def finish(c, _):
        cols = columns(c)
        mine = pl.ds(pl.multiple_of(hz * orows, orows), orows)

        @pl.when(hz == 0)
        def _():
            arrived(c, nh).wait_recv()
            obuf[:, cols] = (ybuf[mine, cols].astype(F32) + rbuf[nh, :, cols].astype(F32)).astype(BF16)

        @pl.when(hz == nh - 1)
        def _():
            arrived(c, hz).wait_recv()
            obuf[:, cols] = (ybuf[mine, cols].astype(F32) + rbuf[hz, :, cols].astype(F32)).astype(BF16)

        @pl.when((hz > 0) & (hz < nh - 1))
        def _():
            arrived(c, hz).wait_recv()
            arrived(c, nh).wait_recv()
            obuf[:, cols] = (ybuf[mine, cols].astype(F32) + rbuf[hz, :, cols].astype(F32)
                             + rbuf[nh, :, cols].astype(F32)).astype(BF16)

        leave(c).start()
        return 0

    lax.fori_loop(0, chunks, finish, 0)

    for k in range(1, chips):
        q_out(k).wait_send()
        q_pass(jnp.int32(2 * k)).wait_send()
    q_mate.wait_send()

    def drain(b, _):
        mate_stat(b).wait_send()
        mate_part(b).wait_send()
        att_part(b, core).wait_send()
        for d in range(1, chips):
            chip_stat(b, d).wait_send()
            chip_part(b, d).wait_send()
        return 0

    lax.fori_loop(0, n, drain, 0)

    def drain_y(c, _):
        for t in range(nh):
            @pl.when(t != hz)
            def _():
                up(c, t).wait_send()
        leave(c).wait()
        return 0

    lax.fori_loop(0, chunks, drain_y, 0)


def per_device(
    n, nh, queries, cache_keys, cache_values, new_keys, new_values, out_weight,
    new_counts, cache_counts, row_dest,
):
    rows, width = queries.shape
    cached, kvw = cache_keys.shape
    kv = kvw // HEAD_DIM
    grp = width // kvw
    depth, cols = out_weight.shape
    keys = cached * 3 // 4 + -(-rows // HEAD_DIM) * HEAD_DIM
    everyone = n * rows
    orows = everyone // nh
    chips = n // 2
    half = width // 2
    plan = parts_of(kv, grp)
    slots = sum(len(items) for items in plan)
    tall = (plan[0][0][2] - plan[0][0][1]) * rows
    cw = 1024 if cols % 1024 == 0 else HEAD_DIM
    chunks = cols // cw
    dma = pltpu.SemaphoreType.DMA
    hbm = pl.BlockSpec(memory_space=pl.ANY)
    smem = pl.BlockSpec(memory_space=pltpu.SMEM)
    vmem = pl.BlockSpec(memory_space=pltpu.VMEM)
    return pl.pallas_call(
        functools.partial(fused, n, nh),
        out_shape=jax.ShapeDtypeStruct((orows, cols), BF16),
        in_specs=[hbm] * 6 + [smem] * 2 + [vmem],
        out_specs=hbm,
        scratch_shapes=[
            pltpu.VMEM((n, rows, width), BF16),
            pltpu.VMEM((keys, kvw), BF16),
            pltpu.VMEM((kv, keys, 2 * HEAD_DIM), BF16),
            pltpu.VMEM((rows, keys), F32),
            pltpu.VMEM((slots, tall, keys), F32),
            pltpu.VMEM((n, 2, rows, half), BF16),
            pltpu.VMEM((n, 2, 8, HEAD_DIM), F32),
            pltpu.VMEM((n, rows, half), BF16),
            pltpu.VMEM((n, 8, HEAD_DIM), F32),
            pltpu.VMEM((n, rows, half), BF16),
            pltpu.VMEM((n, 8, HEAD_DIM), F32),
            pltpu.VMEM((chips - 1, n, rows, half), BF16),
            pltpu.VMEM((chips - 1, n, 8, HEAD_DIM), F32),
            pltpu.VMEM((n, 2, rows, half), BF16),
            pltpu.VMEM((everyone, width), BF16),
            pltpu.VMEM((chunks, depth, cw), BF16),
            pltpu.VMEM((everyone, cw), F32),
            pltpu.VMEM((everyone, cols), BF16),
            pltpu.VMEM((nh + 1, orows, cols), BF16),
            pltpu.VMEM((orows, cols), BF16),
            dma((2,)), dma((kv, 2)), dma((chunks,)), dma,
            dma((n,)), dma((n,)),
            dma((n,)), dma((n,)), dma((n,)), dma((n,)),
            dma((chips - 1, n)), dma((chips - 1, n)), dma((chips - 1, n)), dma((chips - 1, n)),
            dma((n,)), dma((n,)),
            dma((nh + 1, chunks)), dma((nh + 1, chunks)), dma((chunks,)),
        ],
        compiler_params=pltpu.CompilerParams(
            collective_id=0, has_side_effects=True, vmem_limit_bytes=60 * 1024 * 1024),
    )(queries, cache_keys, cache_values, new_keys, new_values, out_weight,
      new_counts, cache_counts, row_dest.reshape(1, everyone))


def solution(mesh):
    n, nh = mesh.shape["ctx"], mesh.shape["head"]
    return jax.shard_map(
        functools.partial(per_device, n, nh),
        mesh=mesh,
        in_specs=(
            P(("groups", "ctx"), "head"),
            P(("groups", "ctx"), "head"),
            P(("groups", "ctx"), "head"),
            P(("groups", "ctx"), "head"),
            P(("groups", "ctx"), "head"),
            P("head", "ctx"),
            P("groups", None),
            P("groups", None),
            P("groups"),
        ),
        out_specs=P(("groups", "head"), "ctx"),
        check_vma=False,
    )
```
